32 devices in a mesh: chan: 16 (over z, y, core), dist: 2 (over x).
Axes of the slice: x: 2, y: 2, z: 4, core: 2. Of those that a mesh axis runs over, the one named last changes fastest.
Arguments:
- q_now: float32 [16384, 256], P('chan', 'dist'), may hold values from -6 to 6
- q_prev: float32 [16384, 256], P('chan', 'dist'), may hold values from -6 to 6
- panels: bfloat16 [4, 16384, 2048], P(None, 'chan'), may hold values from -0.0625 to 0.0625
- col_block: int32 [16, 4], P('chan'), may hold values from 0 to 7, as said below
- lam_index: int32 [16, 4], P('chan'), may hold values from 0 to 7
- energies: float32 [16384], P('chan'), may hold values from -0.4 to 0.4
- radial: float32 [8, 256], P(None, 'dist'), may hold values from -2 to 2
- damping: float32 [256], P('dist'), may hold values from 0.5 to 1
Outputs:
- q_out: float32 [16384, 256], P('chan', 'dist')
- q_last: float32 [16384, 256], P('chan', 'dist')
The draws below stay inside these ranges and needn't reach their ends.
Inputs may be any that keep to these rules, and one draw needn't show every extreme that they name: `col_block`: each row names 4 different column blocks.
All inputs are finite; a program needn't handle non-finite values.
Results may differ from the reference program's by a relative error of at most 0.0027.
Values may be sent and summed in bfloat16 or wider, within the bound.
No kernel may reach another device: no remote copies, remote signals or barrier semaphores. Data moves between devices by JAX's collectives and lax.ppermute only.
A program may use at most 64 MiB of HBM per device.

```python
import jax
import jax.numpy as jnp
from jax import lax

C = 16384
PC = 2048
NPAN = 4
NLAM = 8
KCHEB = 3
NR = 8
CH_DEV = 1024
NCB = 8
NSTRIP = 16
NRT = 32
NPTS = 256


def draw_col_block(key, part):
    base_rows = jnp.tile(jnp.arange(NCB, dtype=jnp.int32)[None, :], (NSTRIP, 1))
    mixed = jax.random.permutation(key, base_rows, axis=1, independent=True)
    return mixed[:, :NPAN]


def plant(values, own_key, low, high):
    spot = [jax.random.randint(jax.random.fold_in(own_key, axis), (), 0, length) for axis, length in enumerate(values.shape)]
    main_axis = values.shape.index(max(values.shape))
    next_to = spot[:main_axis] + [(spot[main_axis] + 1) % values.shape[main_axis]] + spot[main_axis + 1:]
    return values.at[tuple(spot)].set(low).at[tuple(next_to)].set(high)


def shard_levels(key, shape, cuts, low, top_value):
    factor_of, own = 1.0, jax.random.fold_in(key, 6)
    for axis_at, shards_of in cuts:
        heights = jnp.exp(jax.random.uniform(jax.random.fold_in(own, axis_at), (shards_of,), jnp.float32, low / len(cuts), top_value / len(cuts)))
        factor_of = factor_of * jnp.repeat(heights, shape[axis_at] // shards_of).reshape([-1 if axis == axis_at else 1 for axis in range(len(shape))])
    return factor_of


def gaussian(rng, shape, width, reach, shards=(), kind=jnp.bfloat16):
    values = width * jax.random.normal(rng, shape, jnp.float32)
    if shards:
        values = values * shard_levels(rng, shape, shards, -0.22, 0.18)
    return jnp.clip(values, -reach, reach).astype(kind)


def setup_inputs(seed: int = 0) -> dict:
    arg_keys = jax.random.split(jax.random.key(seed), 9)
    q_now = gaussian(arg_keys[0], (C, NPTS), 1.0, 6.0, ((0, 16), (1, 2)), jnp.float32)
    q_prev = gaussian(arg_keys[1], (C, NPTS), 1.0, 6.0, ((0, 16), (1, 2)), jnp.float32)
    panels = gaussian(arg_keys[2], (NPAN, C, PC), (NPAN * PC) ** -0.5, 0.0625, ((1, 16),))
    col_block = draw_col_block(jax.random.fold_in(arg_keys[8], 71), 0)
    lam_index = plant(jax.random.randint(arg_keys[4], (NSTRIP, NPAN), 0, NLAM), jax.random.fold_in(arg_keys[4], 1), 0, NLAM - 1).astype(jnp.int32)
    energies = jnp.clip(jax.random.uniform(arg_keys[5], (C,), jnp.float32, -0.4, 0.4) * shard_levels(arg_keys[5], (C,), ((0, 16),), -0.4, 0.0), -0.4, 0.4)
    radial = gaussian(arg_keys[6], (NLAM, NPTS), 0.3, 2.0, ((1, 2),), jnp.float32)
    damping = jnp.clip(0.5 + 0.5 * jax.random.uniform(arg_keys[7], (NPTS,), jnp.float32) ** shard_levels(arg_keys[7], (NPTS,), ((0, 2),), -0.2, 0.2), 0.5, 1.0)
    return dict(q_now=q_now, q_prev=q_prev, panels=panels, col_block=col_block, lam_index=lam_index, energies=energies, radial=radial, damping=damping)


stencil = (-1.0 / 560.0, 8.0 / 315.0, -0.2, 1.6, -205.0 / 72.0, 1.6, -0.2, 8.0 / 315.0, -1.0 / 560.0)
kinetic_scale = 0.04


def laplacian(states):
    grid_cells = states.reshape(C, NRT, NR)
    pad_big = jnp.pad(grid_cells, ((0, 0), (4, 4), (0, 0)))
    pad_small = jnp.pad(grid_cells, ((0, 0), (0, 0), (4, 4)))
    summed = jnp.zeros_like(grid_cells)
    for tap_index in range(9):
        summed = summed + stencil[tap_index] * (pad_big[:, tap_index:tap_index + NRT, :] + pad_small[:, :, tap_index:tap_index + NR])
    return summed.reshape(C, NPTS)


def coupling(states, panels, col_block, lam_index, radial):
    rounded = lax.optimization_barrier(states.astype(jnp.bfloat16))
    widened = rounded.astype(jnp.float32)

    def strip_rows(strip_idx):
        own_panels = lax.dynamic_slice_in_dim(panels, (strip_idx * CH_DEV).astype(jnp.int32), CH_DEV, 1)
        summed = jnp.zeros((CH_DEV, NPTS), jnp.float32)
        for panel_idx in range(NPAN):
            first_col = (col_block[strip_idx, panel_idx] * PC).astype(jnp.int32)
            columns = lax.dynamic_slice_in_dim(widened, first_col, PC, 0)
            product = jnp.dot(own_panels[panel_idx].astype(jnp.float32), columns, precision=lax.Precision.HIGHEST, preferred_element_type=jnp.float32)
            weight_row = radial[lam_index[strip_idx, panel_idx]]
            summed = summed + weight_row * product
        return summed

    blocks = lax.map(strip_rows, jnp.arange(NSTRIP, dtype=jnp.int32))
    return blocks.reshape(C, NPTS)


def reference(q_now, q_prev, panels, col_block, lam_index, energies, radial, damping):
    current = q_now
    before = q_prev
    for turn_index in range(KCHEB):
        hamilton = -kinetic_scale * laplacian(current) + energies[:, None] * current + coupling(current, panels, col_block, lam_index, radial)
        nextval = damping[None, :] * (2.0 * hamilton - damping[None, :] * before)
        before = current
        current = nextval
    return current, before
```

```python
import jax
import jax.numpy as jnp
import numpy as np
from jax import lax
from jax.experimental import pallas as pl
from jax.experimental.pallas import tpu as pltpu
from jax.sharding import PartitionSpec as P

KCHEB = 3
NR = 8
CORES = 2

stencil = (
    -1.0 / 560.0,
    8.0 / 315.0,
    -0.2,
    1.6,
    -205.0 / 72.0,
    1.6,
    -0.2,
    8.0 / 315.0,
    -1.0 / 560.0,
)
kinetic_scale = 0.04


def ring_order(chips):
    return list(range(0, chips, 2)) + list(range(1, chips, 2))[::-1]


def ring_perm(chips):
    order = ring_order(chips)
    perm = []
    for at in range(chips):
        perm.append((CORES * order[at], CORES * order[(at + 1) % chips]))
        perm.append((CORES * order[at] + 1, CORES * order[(at - 1) % chips] + 1))
    return perm


def chip_at(place, chips):
    half = (chips + 1) // 2
    place = lax.rem(place + 2 * chips, chips)
    return jnp.where(place < half, 2 * place, 2 * (chips - 1 - place) + 1)


def place_of(chip, chips):
    return jnp.where(lax.rem(chip, 2) == 0, lax.div(chip, 2), chips - 1 - lax.div(chip, 2))


def stencil_matrices(points):
    wide = np.zeros((3 * points, points), np.float64)
    for point in range(points):
        for tap, scale in enumerate(stencil):
            scale = -2.0 * kinetic_scale * scale
            wide[points + point + (tap - 4) * NR, point] += scale
            small = point % NR + tap - 4
            if 0 <= small < NR:
                wide[points + point + tap - 4, point] += scale
    mats = np.stack([wide[points : 2 * points], wide[:points], wide[2 * points :]]).astype(np.float32)
    high = mats.astype(jnp.bfloat16)
    low = (mats - high.astype(np.float32)).astype(jnp.bfloat16)
    return jnp.asarray(np.stack([high, low]))


def vmem(x):
    return pltpu.with_memory_space_constraint(x, pltpu.VMEM)


VSPEC = pl.BlockSpec(memory_space=pltpu.VMEM)
SSPEC = pl.BlockSpec(memory_space=pltpu.SMEM)


def stage(chips, sizes, blocks, first, base, last, final):
    rows, points, cols, panels_n, nbrs, dist_n = sizes
    chips_per_block = cols // (CORES * rows)

    def kernel(where, col, lam, panels, radial, damp, *refs):
        refs = list(refs)
        shards = [[refs.pop(0) for _ in range(n)] for _, n in blocks]
        if base:
            cur, before, energy, mats = [refs.pop(0) for _ in range(4)]
            sides = [refs.pop(0) for _ in range(nbrs)]
        if not first:
            refs.pop(0)
        acc = refs.pop(0)
        rounded = refs.pop(0) if last and not final else None
        me = where[0]
        core = lax.rem(me, CORES)
        place = place_of(lax.div(me, CORES), chips)
        way = 1 - 2 * core
        scale = damp[...]

        if first:
            acc[...] = jnp.zeros_like(acc)

        def add(chip, pairs):
            block = lax.div(chip, chips_per_block)
            start = lax.rem(chip, chips_per_block) * (CORES * rows)
            which = jnp.int32(0)
            found = col[0, 0] == block
            for j in range(1, panels_n):
                hit = col[0, j] == block
                which = jnp.where(hit, j, which)
                found = found | hit

            @pl.when(found)
            def _():
                total = None
                for shard, of_core in pairs:
                    off = pl.multiple_of(start + of_core * rows, 128)
                    part = jnp.dot(panels[which, :, pl.ds(off, rows)], shard[...], preferred_element_type=jnp.float32)
                    total = part if total is None else total + part
                weight = 2.0 * scale * radial[pl.ds(lam[0, which], 1), :]
                acc[...] += weight * total

        if base:
            own = cur[...]
            own_high = own.astype(jnp.bfloat16)
            own_low = (own - own_high.astype(jnp.float32)).astype(jnp.bfloat16)

            def lap(high, low, at):
                dot = lambda a, b: jnp.dot(a, b, preferred_element_type=jnp.float32)
                return dot(high, mats[0, at]) + dot(low, mats[0, at]) + dot(high, mats[1, at])

            total = lap(own_high, own_low, 0)
            for i, side in enumerate(sides):
                value = side[...]
                high = value.astype(jnp.bfloat16)
                low = (value - high.astype(jnp.float32)).astype(jnp.bfloat16)
                at = i + 1 if nbrs == 2 else jnp.where(where[1] == 0, 2, 1)
                total = total + lap(high, low, at)
            acc[...] += scale * (total + 2.0 * energy[...] * own - scale * before[...])

        for (distance, n), refs_of in zip(blocks, shards):
            if distance == 0:
                add(lax.div(me, CORES), [(refs_of[0], core), (refs_of[1], 1 - core)])
            elif n == 2:
                add(chip_at(place - way * distance, chips), [(refs_of[0], core), (refs_of[1], 1 - core)])
            else:
                add(chip_at(place - way * distance, chips), [(refs_of[0], core), (refs_of[1], 1 - core)])
                add(chip_at(place + way * distance, chips), [(refs_of[2], 1 - core), (refs_of[3], core)])
        if rounded is not None:
            rounded[...] = acc[...].astype(jnp.bfloat16)

    def call(name, where, col, lam, panels, radial, damp, shards, base_args, acc):
        args = [where, col, lam, vmem(panels), radial, damp] + [vmem(s) for s in shards]
        specs = [SSPEC] * 3 + [VSPEC] * (3 + len(shards))
        if base:
            args += [vmem(a) for a in base_args]
            specs += [VSPEC] * len(base_args)
        alias = {}
        if not first:
            alias = {len(args): 0}
            args.append(vmem(acc))
            specs.append(VSPEC)
        outs = [pltpu.VMEM((rows, points), jnp.float32)]
        if last and not final:
            outs.append(pltpu.VMEM((rows, points), jnp.bfloat16))
        return pl.pallas_call(
            kernel,
            out_shape=outs,
            in_specs=specs,
            out_specs=[VSPEC] * len(outs),
            input_output_aliases=alias,
            compiler_params=pltpu.CompilerParams(vmem_limit_bytes=12 << 20),
            name=name,
        )(*args)

    return call


def local(q_now, q_prev, panels, col_block, lam_index, energies, radial, damping):
    count = lax.axis_size("chan")
    dist_n = lax.axis_size("dist")
    chips = count // CORES
    far = chips // 2
    rows, points = q_now.shape
    cols = panels.shape[2]
    where = jnp.stack([lax.axis_index("chan"), lax.axis_index("dist")]).astype(jnp.int32)
    ring = ring_perm(chips)
    swap = [(i, i ^ 1) for i in range(count)]
    damp = damping[None, :]
    energy = jnp.broadcast_to(energies[:, None], (rows, points))
    mats = stencil_matrices(points)
    right = [(i, i + 1) for i in range(dist_n - 1)]
    left = [(i + 1, i) for i in range(dist_n - 1)]
    nbrs = {1: 0, 2: 1}.get(dist_n, 2)
    sizes = (rows, points, cols, panels.shape[0], nbrs, dist_n)

    def hop(x):
        return lax.ppermute(x, "chan", ring)

    def other(x):
        return lax.ppermute(x, "chan", swap)

    current, before = q_now, q_prev
    rounded = q_now.astype(jnp.bfloat16)
    for turn in range(KCHEB):
        final = turn == KCHEB - 1
        p = hop(rounded)
        partner = other(rounded)
        if nbrs == 0:
            sides = []
        elif nbrs == 1:
            sides = [lax.ppermute(current, "dist", right + left)]
        else:
            sides = [lax.ppermute(current, "dist", right), lax.ppermute(current, "dist", left)]
        base_args = [current, before, energy, mats] + sides
        common = (where, col_block, lam_index, panels, radial, damp)
        q = hop(partner)
        groups = {0: [rounded, partner]}
        for r in range(1, far):
            groups[r] = [p, q, other(p), other(q)]
            p = hop(p)
            if r + 1 < far:
                q = hop(q)
        groups[far] = [p, other(p)]
        acc = None
        for r in range(1, far + 1):
            blocks = [(0, 2), (1, 4)] if r == 1 else [(r, len(groups[r]))]
            shards = [s for d, _ in blocks for s in groups[d]]
            call = stage(chips, sizes, blocks, r == 1, r == 2, r == far, final)
            outs = call(f"step{turn}_{r}", *common, shards, base_args, acc)
            acc = outs[0]
        before, current = current, acc
        if not final:
            rounded = outs[1]
    return (current, before)


def solution(mesh):
    return jax.shard_map(
        local,
        mesh=mesh,
        in_specs=(
            P("chan", "dist"),
            P("chan", "dist"),
            P(None, "chan", None),
            P("chan", None),
            P("chan", None),
            P("chan"),
            P(None, "dist"),
            P("dist"),
        ),
        out_specs=(P("chan", "dist"), P("chan", "dist")),
        check_vma=False,
    )
```

```python
import jax
import jax.numpy as jnp
import numpy as np
from jax import lax
from jax.experimental import pallas as pl
from jax.experimental.pallas import tpu as pltpu
from jax.sharding import PartitionSpec as P


KCHEB = 3
NR = 8
CORES = 2

stencil = (
    -1.0 / 560.0,
    8.0 / 315.0,
    -0.2,
    1.6,
    -205.0 / 72.0,
    1.6,
    -0.2,
    8.0 / 315.0,
    -1.0 / 560.0,
)
kinetic_scale = 0.04


def ring_order(chips):
    return list(range(0, chips, 2)) + list(range(1, chips, 2))[::-1]


def ring_perm(chips):
    order = ring_order(chips)
    perm = []
    for at in range(chips):
        perm.append((CORES * order[at], CORES * order[(at + 1) % chips]))
        perm.append((CORES * order[at] + 1, CORES * order[(at - 1) % chips] + 1))
    return perm


def chip_at(place, chips):
    half = (chips + 1) // 2
    place = lax.rem(place + 2 * chips, chips)
    return jnp.where(place < half, 2 * place, 2 * (chips - 1 - place) + 1)


def place_of(chip, chips):
    return jnp.where(lax.rem(chip, 2) == 0, lax.div(chip, 2), chips - 1 - lax.div(chip, 2))


def stencil_matrices(points):
    wide = np.zeros((3 * points, points), np.float64)
    for point in range(points):
        for tap, scale in enumerate(stencil):
            scale = -2.0 * kinetic_scale * scale
            wide[points + point + (tap - 4) * NR, point] += scale
            small = point % NR + tap - 4
            if 0 <= small < NR:
                wide[points + point + tap - 4, point] += scale
    mats = np.stack([wide[points : 2 * points], wide[:points], wide[2 * points :]]).astype(np.float32)
    high = mats.astype(jnp.bfloat16)
    low = (mats - high.astype(np.float32)).astype(jnp.bfloat16)
    return jnp.asarray(np.stack([high, low]))


def vmem(x):
    return pltpu.with_memory_space_constraint(x, pltpu.VMEM)


VSPEC = pl.BlockSpec(memory_space=pltpu.VMEM)
SSPEC = pl.BlockSpec(memory_space=pltpu.SMEM)
VMEM_BYTES = 12 << 20
OWN, RING, SWAP = 0, -1, 1


def prepare(q_now, where):
    def kernel(where, x, out):
        out[...] = x[...].astype(jnp.bfloat16)

    return pl.pallas_call(
        kernel,
        out_shape=pltpu.VMEM(q_now.shape, jnp.bfloat16),
        in_specs=[SSPEC, VSPEC],
        out_specs=VSPEC,
        cost_estimate=pl.CostEstimate(flops=12 * 10**9, transcendentals=0, bytes_accessed=q_now.size * 6),
        compiler_params=pltpu.CompilerParams(vmem_limit_bytes=VMEM_BYTES),
        name="prepare",
    )(where, q_now)


class Stages:
    def __init__(self, chips, shape, panels, nbrs, common):
        self.chips = chips
        self.rows, self.points = shape
        self.panels_n, _, self.cols = panels.shape
        self.nbrs = nbrs
        self.common = common

    def run(self, parts, acc=None, base=(), out="acc"):
        rows, points, cols, chips = self.rows, self.points, self.cols, self.chips
        chips_per_block = cols // (CORES * rows)
        first = acc is None
        counts = [len(shards) for _, _, shards in parts]

        def kernel(where, col, lam, panels, radial, damp, *refs):
            refs = list(refs)
            shards = [[refs.pop(0) for _ in range(n)] for n in counts]
            terms = [refs.pop(0) for _ in base]
            old = None if first else refs.pop(0)
            new = refs.pop(0)
            rounded = refs.pop(0) if out == "both" else None
            me = where[0]
            core = lax.rem(me, CORES)
            place = place_of(lax.div(me, CORES), chips)
            way = 1 - 2 * core
            scale = damp[...]

            def write(value):
                new[...] = value
                if rounded is not None:
                    rounded[...] = value.astype(jnp.bfloat16)

            if first:
                new[...] = jnp.zeros_like(new)

            if base:
                cur, before, energy, mats = terms[:4]
                own = cur[...]
                values = [own] + [side[...] for side in terms[4:]]
                highs = [v.astype(jnp.bfloat16) for v in values]
                lows = [(v - h.astype(jnp.float32)).astype(jnp.bfloat16) for v, h in zip(values, highs)]
                if self.nbrs == 1:
                    picks = [0, jnp.where(where[1] == 0, 2, 1)]
                else:
                    picks = list(range(len(values)))
                join = lambda xs, axis: jnp.concatenate(xs, axis=axis) if len(xs) > 1 else xs[0]
                mat = [join([mats[i, at] for at in picks], 0) for i in range(2)]
                high, low = join(highs, 1), join(lows, 1)
                dot = lambda a, b: jnp.dot(a, b, preferred_element_type=jnp.float32)
                total = dot(high, mat[0]) + dot(low, mat[0]) + dot(high, mat[1])
                new[...] = old[...] + scale * (total + 2.0 * energy[...] * own - scale * before[...])
                old = new

            for at, ((side, distance, described), shard_refs) in enumerate(zip(parts, shards)):
                if side == OWN:
                    chip = lax.div(me, CORES)
                else:
                    chip = chip_at(place + side * way * distance, chips)
                block = lax.div(chip, chips_per_block)
                start = lax.rem(chip, chips_per_block) * (CORES * rows)
                which = jnp.int32(0)
                found = col[0, 0] == block
                for j in range(1, self.panels_n):
                    hit = col[0, j] == block
                    which = jnp.where(hit, j, which)
                    found = found | hit
                source = new if first or base or at else old

                @pl.when(found)
                def _():
                    total = None
                    for (whose, _), shard in zip(described, shard_refs):
                        of_core = core if whose == 0 else 1 - core
                        off = pl.multiple_of(start + of_core * rows, 128)
                        part = jnp.dot(panels[which, :, pl.ds(off, rows)], shard[...], preferred_element_type=jnp.float32)
                        total = part if total is None else total + part
                    weight = 2.0 * scale * radial[pl.ds(lam[0, which], 1), :]
                    value = source[...] + weight * total
                    if at == len(parts) - 1:
                        write(value)
                    else:
                        new[...] = value

                if out != "acc" and at == len(parts) - 1:

                    @pl.when(jnp.logical_not(found))
                    def _():
                        write(source[...])

        where, col, lam, panels, radial, damp = self.common
        args = [where, col, lam, vmem(panels), radial, damp]
        specs = [SSPEC] * 3 + [VSPEC] * 3
        for x in [shard for _, _, shards in parts for _, shard in shards] + list(base):
            args.append(vmem(x))
            specs.append(VSPEC)
        alias = {}
        if not first:
            if out != "final":
                alias = {len(args): 0}
            args.append(vmem(acc))
            specs.append(VSPEC)
        if out == "final":
            outs = [jax.ShapeDtypeStruct((rows, points), jnp.float32)]
        else:
            outs = [pltpu.VMEM((rows, points), jnp.float32)]
        if out == "both":
            outs.append(pltpu.VMEM((rows, points), jnp.bfloat16))
        products = sum(counts)
        done = pl.pallas_call(
            kernel,
            out_shape=outs,
            in_specs=specs,
            out_specs=[VSPEC] * len(outs),
            input_output_aliases=alias,
            cost_estimate=pl.CostEstimate(
                flops=products * rows * rows * points, transcendentals=0, bytes_accessed=rows * points * 8
            ),
            compiler_params=pltpu.CompilerParams(vmem_limit_bytes=VMEM_BYTES),
        )(*args)
        return done if len(done) > 1 else done[0]


def local(q_now, q_prev, panels, col_block, lam_index, energies, radial, damping):
    count = lax.axis_size("chan")
    dist_n = lax.axis_size("dist")
    chips = count // CORES
    far = chips // 2
    rows, points = q_now.shape
    where = jnp.stack([lax.axis_index("chan"), lax.axis_index("dist")]).astype(jnp.int32)
    ring = ring_perm(chips)
    swap = [(i, i ^ 1) for i in range(count)]
    energy = jnp.broadcast_to(energies[:, None], (rows, points))
    mats = stencil_matrices(points)
    right = [(i, i + 1) for i in range(dist_n - 1)]
    left = [(i + 1, i) for i in range(dist_n - 1)]
    if dist_n == 1:
        shifts = []
    elif dist_n == 2:
        shifts = [right + left]
    else:
        shifts = [right, left]
    common = (where, col_block, lam_index, panels, radial, damping[None, :])
    stages = Stages(chips, (rows, points), panels, len(shifts), common)

    current, before = q_now, q_prev
    rounded = prepare(q_now, where)
    for turn in range(KCHEB):
        final = turn == KCHEB - 1
        p = lax.ppermute(rounded, "chan", ring)
        partner = lax.ppermute(rounded, "chan", swap)
        sides = [lax.ppermute(current, "dist", perm) for perm in shifts]
        q = lax.ppermute(partner, "chan", ring)
        acc = stages.run([(OWN, 0, ((0, rounded), (1, partner)))])
        for r in range(1, far):
            next_p = lax.ppermute(p, "chan", ring)
            swap_p = lax.ppermute(p, "chan", swap)
            if r + 1 < far:
                next_q = lax.ppermute(q, "chan", ring)
            swap_q = lax.ppermute(q, "chan", swap)
            parts = [(RING, r, ((0, p), (1, q))), (SWAP, r, ((1, swap_p), (0, swap_q)))]
            if r + 1 == far:
                acc = stages.run([], acc, [current, before, energy, mats] + sides)
            acc = stages.run(parts, acc)
            p, q = next_p, next_q
        swap_p = lax.ppermute(p, "chan", swap)
        acc = stages.run([(RING, far, ((0, p),))], acc)
        done = stages.run([(SWAP, far, ((1, swap_p),))], acc, out="final" if final else "both")
        before = current
        if final:
            current = done
        else:
            current, rounded = done
    return (current, before)


def solution(mesh):
    return jax.shard_map(
        local,
        mesh=mesh,
        in_specs=(
            P("chan", "dist"),
            P("chan", "dist"),
            P(None, "chan", None),
            P("chan", None),
            P("chan", None),
            P("chan"),
            P(None, "dist"),
            P("dist"),
        ),
        out_specs=(P("chan", "dist"), P("chan", "dist")),
        check_vma=False,
    )
```

```python
import jax
import jax.numpy as jnp
import numpy as np
from jax import lax
from jax.experimental import pallas as pl
from jax.experimental.pallas import tpu as pltpu
from jax.sharding import PartitionSpec as P


KCHEB = 3
NR = 8
CORES = 2

stencil = (
    -1.0 / 560.0,
    8.0 / 315.0,
    -0.2,
    1.6,
    -205.0 / 72.0,
    1.6,
    -0.2,
    8.0 / 315.0,
    -1.0 / 560.0,
)
kinetic_scale = 0.04


def ring_order(chips):
    return list(range(0, chips, 2)) + list(range(1, chips, 2))[::-1]


def ring_perm(chips):
    order = ring_order(chips)
    perm = []
    for at in range(chips):
        perm.append((CORES * order[at], CORES * order[(at + 1) % chips]))
        perm.append((CORES * order[at] + 1, CORES * order[(at - 1) % chips] + 1))
    return perm


def chip_at(place, chips):
    half = (chips + 1) // 2
    place = lax.rem(place + 2 * chips, chips)
    return jnp.where(place < half, 2 * place, 2 * (chips - 1 - place) + 1)


def place_of(chip, chips):
    return jnp.where(lax.rem(chip, 2) == 0, lax.div(chip, 2), chips - 1 - lax.div(chip, 2))


def stencil_matrices(points):
    wide = np.zeros((3 * points, points), np.float64)
    for point in range(points):
        for tap, scale in enumerate(stencil):
            scale = -2.0 * kinetic_scale * scale
            wide[points + point + (tap - 4) * NR, point] += scale
            small = point % NR + tap - 4
            if 0 <= small < NR:
                wide[points + point + tap - 4, point] += scale
    mats = np.stack([wide[points : 2 * points], wide[:points], wide[2 * points :]]).astype(np.float32)
    high = mats.astype(jnp.bfloat16)
    low = (mats - high.astype(np.float32)).astype(jnp.bfloat16)
    return jnp.asarray(np.stack([high, low]))


def vmem(x):
    return pltpu.with_memory_space_constraint(x, pltpu.VMEM)


def smem(x):
    return pltpu.with_memory_space_constraint(x, pltpu.SMEM)


VSPEC = pl.BlockSpec(memory_space=pltpu.VMEM)
SSPEC = pl.BlockSpec(memory_space=pltpu.SMEM)
VMEM_BYTES = 12 << 20
FIELDS = 3


def slots(chips):
    far = chips // 2
    near = [(side, r) for r in range(1, far) for side in (-1, 1)]
    return [(0, 0)] + near + [(-1, far)]


def prepare(q_now):
    def kernel(x, out, rounded):
        value = x[...]
        out[...] = value
        rounded[...] = value.astype(jnp.bfloat16)

    return pl.pallas_call(
        kernel,
        out_shape=[pltpu.VMEM(q_now.shape, q_now.dtype), pltpu.VMEM(q_now.shape, jnp.bfloat16)],
        in_specs=[VSPEC],
        out_specs=[VSPEC, VSPEC],
        cost_estimate=pl.CostEstimate(flops=40 * 10**9, transcendentals=0, bytes_accessed=q_now.size * 6),
        compiler_params=pltpu.CompilerParams(vmem_limit_bytes=VMEM_BYTES),
        name="prepare",
    )(q_now)


def scalars(col_block, lam_index, chips, rows, cols):
    chips_per_block = cols // (CORES * rows)
    table = slots(chips)

    def kernel(col, lam, info):
        me = lax.axis_index("chan").astype(jnp.int32)
        core = lax.rem(me, CORES)
        own = lax.div(me, CORES)
        place = place_of(own, chips)
        way = 1 - 2 * core
        info[0] = core
        info[1] = lax.axis_index("dist").astype(jnp.int32)
        for slot, (side, distance) in enumerate(table):
            chip = own if side == 0 else chip_at(place + side * way * distance, chips)
            block = lax.div(chip, chips_per_block)
            which = jnp.int32(-1)
            level = jnp.int32(0)
            for j in range(col_block.shape[1]):
                hit = col[0, j] == block
                which = jnp.where(hit, j, which)
                level = jnp.where(hit, lam[0, j], level)
            info[2 + FIELDS * slot] = which
            info[3 + FIELDS * slot] = level
            info[4 + FIELDS * slot] = lax.rem(chip, chips_per_block) * (CORES * rows)

    return pl.pallas_call(
        kernel,
        out_shape=pltpu.SMEM((2 + FIELDS * len(table),), jnp.int32),
        in_specs=[SSPEC] * 2,
        out_specs=SSPEC,
        compiler_params=pltpu.CompilerParams(vmem_limit_bytes=VMEM_BYTES),
        name="scalars",
    )(col_block, lam_index)


def store(x):
    def kernel(x, out):
        out[...] = x[...]

    return pl.pallas_call(
        kernel,
        out_shape=jax.ShapeDtypeStruct(x.shape, x.dtype),
        in_specs=[VSPEC],
        out_specs=VSPEC,
        compiler_params=pltpu.CompilerParams(vmem_limit_bytes=VMEM_BYTES),
    )(vmem(x))


class Stages:
    def __init__(self, chips, shape, nbrs, common):
        self.table = slots(chips)
        self.rows, self.points = shape
        self.nbrs = nbrs
        self.common = common

    def run(self, parts, acc=None, base=(), out="acc"):
        rows, points = self.rows, self.points
        first = acc is None
        counts = [len(shards) for _, _, shards in parts]

        def kernel(info, panels, radial, damp, *refs):
            refs = list(refs)
            shards = [[refs.pop(0) for _ in range(n)] for n in counts]
            terms = [refs.pop(0) for _ in base]
            old = None if first else refs.pop(0)
            new = refs.pop(0)
            rounded = refs.pop(0) if out == "both" else None
            core = info[0]
            scale = damp[...]

            def write(value):
                new[...] = value
                if rounded is not None:
                    rounded[...] = value.astype(jnp.bfloat16)

            if base:
                cur, before, energy, mats = terms[:4]
                own = cur[...]
                values = [own] + [side[...] for side in terms[4:]]
                highs = [v.astype(jnp.bfloat16) for v in values]
                lows = [(v - h.astype(jnp.float32)).astype(jnp.bfloat16) for v, h in zip(values, highs)]
                if self.nbrs == 1:
                    picks = [0, jnp.where(info[1] == 0, 2, 1)]
                else:
                    picks = list(range(len(values)))
                join = lambda xs, axis: jnp.concatenate(xs, axis=axis) if len(xs) > 1 else xs[0]
                mat = [join([mats[i, at] for at in picks], 0) for i in range(2)]
                high, low = join(highs, 1), join(lows, 1)
                dot = lambda a, b: jnp.dot(a, b, preferred_element_type=jnp.float32)
                total = dot(high, mat[0]) + dot(low, mat[0]) + dot(high, mat[1])
                new[...] = old[...] + scale * (total + 2.0 * energy[...] * own - scale * before[...])
                old = new

            for at, ((side, distance, described), shard_refs) in enumerate(zip(parts, shards)):
                slot = self.table.index((side, distance))
                which = info[2 + FIELDS * slot]
                level = info[3 + FIELDS * slot]
                start = info[4 + FIELDS * slot]
                found = which >= 0
                source = new if base or at else old
                end = at == len(parts) - 1

                @pl.when(found)
                def _():
                    total = None
                    for (whose, _), shard in zip(described, shard_refs):
                        of_core = core if whose == 0 else 1 - core
                        off = pl.multiple_of(start + of_core * rows, 128)
                        part = jnp.dot(panels[which, :, pl.ds(off, rows)], shard[...], preferred_element_type=jnp.float32)
                        total = part if total is None else total + part
                    value = 2.0 * scale * radial[pl.ds(level, 1), :] * total
                    if source is not None:
                        value = source[...] + value
                    if end:
                        write(value)
                    else:
                        new[...] = value

                if source is None or (out != "acc" and end):

                    @pl.when(jnp.logical_not(found))
                    def _():
                        write(jnp.zeros_like(new) if source is None else source[...])

        info, panels, radial, damp = self.common
        args = [smem(info), vmem(panels), vmem(radial), vmem(damp)]
        specs = [SSPEC] + [VSPEC] * 3
        for x in [shard for _, _, shards in parts for _, shard in shards] + list(base):
            args.append(vmem(x))
            specs.append(VSPEC)
        alias = {}
        if not first:
            if out != "final":
                alias = {len(args): 0}
            args.append(vmem(acc))
            specs.append(VSPEC)
        if out == "final":
            outs = [jax.ShapeDtypeStruct((rows, points), jnp.float32)]
        else:
            outs = [pltpu.VMEM((rows, points), jnp.float32)]
        if out == "both":
            outs.append(pltpu.VMEM((rows, points), jnp.bfloat16))
        products = sum(counts)
        done = pl.pallas_call(
            kernel,
            out_shape=outs,
            in_specs=specs,
            out_specs=[VSPEC] * len(outs),
            input_output_aliases=alias,
            cost_estimate=pl.CostEstimate(
                flops=products * rows * rows * points, transcendentals=0, bytes_accessed=rows * points * 8
            ),
            compiler_params=pltpu.CompilerParams(vmem_limit_bytes=VMEM_BYTES),
        )(*args)
        return done if len(done) > 1 else done[0]


def local(q_now, q_prev, panels, col_block, lam_index, energies, radial, damping):
    count = lax.axis_size("chan")
    dist_n = lax.axis_size("dist")
    chips = count // CORES
    far = chips // 2
    rows, points = q_now.shape
    ring = ring_perm(chips)
    swap = [(i, i ^ 1) for i in range(count)]
    energy = jnp.broadcast_to(energies[:, None], (rows, points))
    mats = stencil_matrices(points)
    right = [(i, i + 1) for i in range(dist_n - 1)]
    left = [(i + 1, i) for i in range(dist_n - 1)]
    if dist_n == 1:
        shifts = []
    elif dist_n == 2:
        shifts = [right + left]
    else:
        shifts = [right, left]
    start, rounded = prepare(q_now)
    info = scalars(col_block, lam_index, chips, rows, panels.shape[2])
    stages = Stages(chips, (rows, points), len(shifts), (info, panels, radial, damping[None, :]))

    def send(x, axis, perm):
        return lax.ppermute(x, axis, perm)

    current, before = start, q_prev
    kept = None
    for turn in range(KCHEB):
        final = turn == KCHEB - 1
        have = {"rounded": rounded}
        acc = None
        for token in plan(far, len(shifts), final):
            kind, r = token[0], token[1]
            if kind == "p":
                have[f"p{r}"] = send(have[f"p{r - 1}"] if r > 1 else rounded, "chan", ring)
            elif kind == "q":
                have[f"q{r}"] = send(have[f"q{r - 1}"] if r > 1 else have["sp0"], "chan", ring)
            elif kind == "sp":
                have[f"sp{r}"] = send(have[f"p{r}"] if r else rounded, "chan", swap)
            elif kind == "sq":
                have[f"sq{r}"] = send(have[f"q{r}"], "chan", swap)
            elif kind == "h":
                have[f"h{r}"] = send(current, "dist", shifts[r])
            elif kind == "k":
                acc = stages.run([(0, 0, ((0, rounded), (1, have["sp0"])))], acc)
            elif kind == "r":
                acc = stages.run([(-1, r, ((0, have[f"p{r}"]), (1, have[f"q{r}"])))], acc)
            elif kind == "s":
                parts = [(1, r, ((1, have[f"sp{r}"]), (0, have[f"sq{r}"])))]
                if r + 1 == far:
                    parts.append((-1, far, ((0, have[f"p{far}"]),)))
                acc = stages.run(parts, acc)
            elif kind == "b":
                sides = [have[f"h{i}"] for i in range(len(shifts))]
                acc = stages.run([], acc, [current, before, energy, mats] + sides)
            elif kind == "o":
                kept = store(current)
            elif kind == "e":
                parts = [(-1, far, ((1, have[f"sp{far}"]),))]
                done = stages.run(parts, acc, out="final" if final else "both")
        before = current
        if final:
            current = done
        else:
            current, rounded = done
    return (current, kept)


def plan(far, shifts, final):
    order = [("p", 1), ("sp", 0)] + [("h", i) for i in range(shifts)] + [("q", 1), ("k", 0)]
    for r in range(1, far):
        early = True
        late = not (True)
        order += [("p", r + 1), ("sp", r)]
        if r > 1:
            if late:
                order.append(("r", r - 1))
            order.append(("s", r - 1))
        if r + 1 < far:
            order.append(("q", r + 1))
        order.append(("sq", r))
        if r + 1 == far:
            order.append(("b", 0))
            order.append(("r", r))
        elif early:
            order.append(("r", r))
    if final:
        order.append(("o", 0))
    return order + [("sp", far), ("s", far - 1), ("e", 0)]


def solution(mesh):
    return jax.shard_map(
        local,
        mesh=mesh,
        in_specs=(
            P("chan", "dist"),
            P("chan", "dist"),
            P(None, "chan", None),
            P("chan", None),
            P("chan", None),
            P("chan"),
            P(None, "dist"),
            P("dist"),
        ),
        out_specs=(P("chan", "dist"), P("chan", "dist")),
        check_vma=False,
    )
```

```python
import jax
import jax.numpy as jnp
import numpy as np
from jax import lax
from jax.experimental import pallas as pl
from jax.experimental.pallas import tpu as pltpu
from jax.sharding import PartitionSpec as P


KCHEB = 3
NR = 8
CORES = 2

stencil = (
    -1.0 / 560.0,
    8.0 / 315.0,
    -0.2,
    1.6,
    -205.0 / 72.0,
    1.6,
    -0.2,
    8.0 / 315.0,
    -1.0 / 560.0,
)
kinetic_scale = 0.04


def ring_order(chips):
    return list(range(0, chips, 2)) + list(range(1, chips, 2))[::-1]


def ring_perm(chips):
    order = ring_order(chips)
    perm = []
    for at in range(chips):
        perm.append((CORES * order[at], CORES * order[(at + 1) % chips]))
        perm.append((CORES * order[at] + 1, CORES * order[(at - 1) % chips] + 1))
    return perm


def chip_at(place, chips):
    half = (chips + 1) // 2
    place = lax.rem(place + 2 * chips, chips)
    return jnp.where(place < half, 2 * place, 2 * (chips - 1 - place) + 1)


def place_of(chip, chips):
    return jnp.where(lax.rem(chip, 2) == 0, lax.div(chip, 2), chips - 1 - lax.div(chip, 2))


def stencil_matrices(points):
    wide = np.zeros((3 * points, points), np.float64)
    for point in range(points):
        for tap, scale in enumerate(stencil):
            scale = -2.0 * kinetic_scale * scale
            wide[points + point + (tap - 4) * NR, point] += scale
            small = point % NR + tap - 4
            if 0 <= small < NR:
                wide[points + point + tap - 4, point] += scale
    mats = np.stack([wide[points : 2 * points], wide[:points], wide[2 * points :]]).astype(np.float32)
    high = mats.astype(jnp.bfloat16)
    low = (mats - high.astype(np.float32)).astype(jnp.bfloat16)
    return jnp.asarray(np.stack([high, low]))


def vmem(x):
    return pltpu.with_memory_space_constraint(x, pltpu.VMEM)


def smem(x):
    return pltpu.with_memory_space_constraint(x, pltpu.SMEM)


VSPEC = pl.BlockSpec(memory_space=pltpu.VMEM)
SSPEC = pl.BlockSpec(memory_space=pltpu.SMEM)
VMEM_BYTES = 12 << 20
FIELDS = 3


def slots(chips):
    far = chips // 2
    near = [(side, r) for r in range(1, far) for side in (-1, 1)]
    return [(0, 0)] + near + [(-1, far)]


def prepare(q_now):
    def kernel(x, out, rounded):
        value = x[...]
        out[...] = value
        rounded[...] = value.astype(jnp.bfloat16)

    return pl.pallas_call(
        kernel,
        out_shape=[pltpu.VMEM(q_now.shape, q_now.dtype), pltpu.VMEM(q_now.shape, jnp.bfloat16)],
        in_specs=[VSPEC],
        out_specs=[VSPEC, VSPEC],
        cost_estimate=pl.CostEstimate(flops=40 * 10**9, transcendentals=0, bytes_accessed=q_now.size * 6),
        compiler_params=pltpu.CompilerParams(vmem_limit_bytes=VMEM_BYTES),
        name="prepare",
    )(q_now)


def scalars(col_block, lam_index, chips, rows, cols):
    chips_per_block = cols // (CORES * rows)
    table = slots(chips)

    def kernel(col, lam, info):
        me = lax.axis_index("chan").astype(jnp.int32)
        core = lax.rem(me, CORES)
        own = lax.div(me, CORES)
        place = place_of(own, chips)
        way = 1 - 2 * core
        info[0] = core
        info[1] = lax.axis_index("dist").astype(jnp.int32)
        for slot, (side, distance) in enumerate(table):
            chip = own if side == 0 else chip_at(place + side * way * distance, chips)
            block = lax.div(chip, chips_per_block)
            which = jnp.int32(-1)
            level = jnp.int32(0)
            for j in range(col_block.shape[1]):
                hit = col[0, j] == block
                which = jnp.where(hit, j, which)
                level = jnp.where(hit, lam[0, j], level)
            info[2 + FIELDS * slot] = which
            info[3 + FIELDS * slot] = level
            info[4 + FIELDS * slot] = lax.rem(chip, chips_per_block) * (CORES * rows)

    return pl.pallas_call(
        kernel,
        out_shape=pltpu.SMEM((2 + FIELDS * len(table),), jnp.int32),
        in_specs=[SSPEC] * 2,
        out_specs=SSPEC,
        compiler_params=pltpu.CompilerParams(vmem_limit_bytes=VMEM_BYTES),
        name="scalars",
    )(col_block, lam_index)


def store(x):
    def kernel(x, out):
        out[...] = x[...]

    return pl.pallas_call(
        kernel,
        out_shape=jax.ShapeDtypeStruct(x.shape, x.dtype),
        in_specs=[VSPEC],
        out_specs=VSPEC,
        compiler_params=pltpu.CompilerParams(vmem_limit_bytes=VMEM_BYTES),
    )(vmem(x))


class Stages:
    def __init__(self, chips, shape, nbrs, common):
        self.table = slots(chips)
        self.rows, self.points = shape
        self.nbrs = nbrs
        self.common = common

    def run(self, parts, acc=None, base=(), out="acc"):
        rows, points = self.rows, self.points
        first = acc is None
        counts = [len(shards) for _, _, shards in parts]

        def kernel(info, panels, radial, damp, *refs):
            refs = list(refs)
            shards = [[refs.pop(0) for _ in range(n)] for n in counts]
            terms = [refs.pop(0) for _ in base]
            old = None if first else refs.pop(0)
            new = refs.pop(0)
            rounded = refs.pop(0) if out == "both" else None
            core = info[0]
            scale = damp[...]

            def write(value):
                new[...] = value
                if rounded is not None:
                    rounded[...] = value.astype(jnp.bfloat16)

            if base:
                cur, before, energy, mats = terms[:4]
                own = cur[...]
                values = [own] + [side[...] for side in terms[4:]]
                highs = [v.astype(jnp.bfloat16) for v in values]
                lows = [(v - h.astype(jnp.float32)).astype(jnp.bfloat16) for v, h in zip(values, highs)]
                if self.nbrs == 1:
                    picks = [0, jnp.where(info[1] == 0, 2, 1)]
                else:
                    picks = list(range(len(values)))
                join = lambda xs, axis: jnp.concatenate(xs, axis=axis) if len(xs) > 1 else xs[0]
                mat = [join([mats[i, at] for at in picks], 0) for i in range(2)]
                high, low = join(highs, 1), join(lows, 1)
                dot = lambda a, b: jnp.dot(a, b, preferred_element_type=jnp.float32)
                total = dot(high, mat[0]) + dot(low, mat[0]) + dot(high, mat[1])
                new[...] = old[...] + scale * (total + 2.0 * energy[...] * own - scale * before[...])
                old = new

            for at, ((side, distance, described), shard_refs) in enumerate(zip(parts, shards)):
                slot = self.table.index((side, distance))
                which = info[2 + FIELDS * slot]
                level = info[3 + FIELDS * slot]
                start = info[4 + FIELDS * slot]
                found = which >= 0
                source = new if base or at else old
                end = at == len(parts) - 1

                @pl.when(found)
                def _():
                    total = None
                    for (whose, _), shard in zip(described, shard_refs):
                        of_core = core if whose == 0 else 1 - core
                        off = pl.multiple_of(start + of_core * rows, 128)
                        part = jnp.dot(panels[which, :, pl.ds(off, rows)], shard[...], preferred_element_type=jnp.float32)
                        total = part if total is None else total + part
                    value = 2.0 * scale * radial[pl.ds(level, 1), :] * total
                    if source is not None:
                        value = source[...] + value
                    if end:
                        write(value)
                    else:
                        new[...] = value

                if source is None or (out != "acc" and end):

                    @pl.when(jnp.logical_not(found))
                    def _():
                        write(jnp.zeros_like(new) if source is None else source[...])

        info, panels, radial, damp = self.common
        args = [smem(info), vmem(panels), vmem(radial), vmem(damp)]
        specs = [SSPEC] + [VSPEC] * 3
        for x in [shard for _, _, shards in parts for _, shard in shards] + list(base):
            args.append(vmem(x))
            specs.append(VSPEC)
        alias = {}
        if not first:
            if out != "final":
                alias = {len(args): 0}
            args.append(vmem(acc))
            specs.append(VSPEC)
        if out == "final":
            outs = [jax.ShapeDtypeStruct((rows, points), jnp.float32)]
        else:
            outs = [pltpu.VMEM((rows, points), jnp.float32)]
        if out == "both":
            outs.append(pltpu.VMEM((rows, points), jnp.bfloat16))
        products = sum(counts)
        done = pl.pallas_call(
            kernel,
            out_shape=outs,
            in_specs=specs,
            out_specs=[VSPEC] * len(outs),
            input_output_aliases=alias,
            cost_estimate=pl.CostEstimate(
                flops=products * rows * rows * points, transcendentals=0, bytes_accessed=rows * points * 8
            ),
            compiler_params=pltpu.CompilerParams(vmem_limit_bytes=VMEM_BYTES),
        )(*args)
        return done if len(done) > 1 else done[0]


def local(q_now, q_prev, panels, col_block, lam_index, energies, radial, damping):
    count = lax.axis_size("chan")
    dist_n = lax.axis_size("dist")
    chips = count // CORES
    far = chips // 2
    rows, points = q_now.shape
    ring = ring_perm(chips)
    swap = [(i, i ^ 1) for i in range(count)]
    energy = jnp.broadcast_to(energies[:, None], (rows, points))
    mats = stencil_matrices(points)
    right = [(i, i + 1) for i in range(dist_n - 1)]
    left = [(i + 1, i) for i in range(dist_n - 1)]
    if dist_n == 1:
        shifts = []
    elif dist_n == 2:
        shifts = [right + left]
    else:
        shifts = [right, left]
    start, rounded = prepare(q_now)
    info = scalars(col_block, lam_index, chips, rows, panels.shape[2])
    stages = Stages(chips, (rows, points), len(shifts), (info, panels, radial, damping[None, :]))

    def send(x, axis, perm):
        return lax.ppermute(x, axis, perm)

    current, before = start, q_prev
    kept = None
    for turn in range(KCHEB):
        final = turn == KCHEB - 1
        have = {"rounded": rounded}
        acc = None
        for token in plan(far, len(shifts), final):
            kind, r = token[0], token[1]
            if kind == "p":
                have[f"p{r}"] = send(have[f"p{r - 1}"] if r > 1 else rounded, "chan", ring)
            elif kind == "q":
                have[f"q{r}"] = send(have[f"q{r - 1}"] if r > 1 else have["sp0"], "chan", ring)
            elif kind == "sp":
                have[f"sp{r}"] = send(have[f"p{r}"] if r else rounded, "chan", swap)
            elif kind == "sq":
                have[f"sq{r}"] = send(have[f"q{r}"], "chan", swap)
            elif kind == "h":
                have[f"h{r}"] = send(current, "dist", shifts[r])
            elif kind == "k":
                acc = stages.run([(0, 0, ((0, rounded), (1, have["sp0"])))], acc)
            elif kind == "r":
                acc = stages.run([(-1, r, ((0, have[f"p{r}"]), (1, have[f"q{r}"])))], acc)
            elif kind == "s":
                acc = stages.run([(1, r, ((1, have[f"sp{r}"]), (0, have[f"sq{r}"])))], acc)
            elif kind == "f":
                acc = stages.run([(-1, r, ((0, have[f"p{r}"]),))], acc)
            elif kind == "b":
                sides = [have[f"h{i}"] for i in range(len(shifts))]
                acc = stages.run([], acc, [current, before, energy, mats] + sides)
            elif kind == "o":
                kept = store(current)
            elif kind == "e":
                parts = [(-1, far, ((1, have[f"sp{far}"]),))]
                done = stages.run(parts, acc, out="final" if final else "both")
        before = current
        if final:
            current = done
        else:
            current, rounded = done
    return (current, kept)


def plan(far, shifts, final):
    order = [("p", 1), ("sp", 0)] + [("h", i) for i in range(shifts)] + [("q", 1), ("k", 0)]
    for r in range(1, far):
        early = True
        late = not (True)
        order += [("p", r + 1), ("sp", r)]
        if r > 1:
            if late:
                order.append(("r", r - 1))
            order.append(("s", r - 1))
        if r + 1 < far:
            order.append(("q", r + 1))
        order.append(("sq", r))
        if r + 1 == far:
            order.append(("b", 0))
            order.append(("r", r))
        elif early:
            order.append(("r", r))
    if final:
        order.append(("o", 0))
    order.append(("s", far - 1))
    return order + [("sp", far), ("f", far), ("e", 0)]


def solution(mesh):
    return jax.shard_map(
        local,
        mesh=mesh,
        in_specs=(
            P("chan", "dist"),
            P("chan", "dist"),
            P(None, "chan", None),
            P("chan", None),
            P("chan", None),
            P("chan"),
            P(None, "dist"),
            P("dist"),
        ),
        out_specs=(P("chan", "dist"), P("chan", "dist")),
        check_vma=False,
    )
```
